256 devices in a mesh: tm: 32 (over x, z), tensor: 8 (over y, core).
Axes of the slice: x: 4, y: 4, z: 8, core: 2. Of those that a mesh axis runs over, the one named last changes fastest.
Arguments:
- latents: float32 [32, 640, 64], P('tm', 'tensor'), may hold values from -6 to 6
- residual: bfloat16 [32, 640, 5120], P('tm'), may hold values from -6 to 6
- timesteps: int32 [32], P('tm'), may hold values from 0 to 999
- step_sizes: float32 [32], P('tm'), may hold values from 0.015 to 0.06
- embed_weight: bfloat16 [64, 5120], replicated
- mod_weight: bfloat16 [3, 256, 5120], P(None, None, 'tensor'), may hold values from -0.75 to 0.75
- up_weight: bfloat16 [5120, 7168], P('tm', 'tensor'), may hold values from -0.078125 to 0.078125
- down_weight: bfloat16 [7168, 5120], P('tensor', 'tm'), may hold values from -0.0625 to 0.0625
- head_weight: bfloat16 [5120, 64], replicated, may hold values from -0.078125 to 0.078125
Outputs:
- drift: float32 [32, 640, 64], P('tm', 'tensor')
- new_latents: float32 [32, 640, 64], P('tm', 'tensor')
The draws below stay inside these ranges and needn't reach their ends.
All inputs are finite; a program needn't handle non-finite values.
Results may differ from the reference program's by a relative error of at most 0.0085.
Values may be sent and summed in bfloat16 or wider, within the bound.
No kernel may reach another device: no remote copies, remote signals or barrier semaphores. Data moves between devices by JAX's collectives and lax.ppermute only.
A program may use at most 128 MiB of HBM per device.

```python
import math
import jax
import jax.numpy as jnp
from jax import lax

D = 5120
FF = 7168
C = 64
FREQ = 256
S = 640
STEPS = 32
N_TENSOR = 8


def draw_embed_weight(key, part):
    first = jax.random.fold_in(key, 11)
    second = jax.random.fold_in(key, 12)
    values = jax.random.normal(first, (C, D), jnp.float32)
    scales = jnp.exp(jax.random.uniform(second, (1, D), jnp.float32, 0.0, math.log(10.0)))
    values = values * scales / 4.0
    return (values / math.sqrt(C)).astype(jnp.bfloat16)


def with_ends(values, rng, low, high):
    spot = [jax.random.randint(jax.random.fold_in(rng, axis), (), 0, length) for axis, length in enumerate(values.shape)]
    widest = values.shape.index(max(values.shape))
    next_to = spot[:widest] + [(spot[widest] + 1) % values.shape[widest]] + spot[widest + 1:]
    return values.at[tuple(spot)].set(low).at[tuple(next_to)].set(high)


def block_levels(rng, extent, pieces, least, high):
    level = 1.0
    for axis_at, shards_of in pieces:
        heights = jax.random.uniform(jax.random.fold_in(jax.random.fold_in(rng, 6), axis_at), (shards_of,), jnp.float32, least / len(pieces), high / len(pieces))
        level = level * jnp.repeat(jnp.exp(heights), extent[axis_at] // shards_of).reshape((-1,) + (1,) * (len(extent) - 1 - axis_at))
    return level


def centred(own_key, dims, deviation, limit, split=(), held_as=jnp.bfloat16):
    array = jax.random.normal(own_key, dims, jnp.float32) * deviation
    if len(split) > 0:
        array = block_levels(own_key, dims, split, -0.22, 0.18) * array
    return jnp.clip(array, min=-limit, max=limit).astype(held_as)


def setup_inputs(seed: int = 0) -> dict:
    key_list = jax.random.split(jax.random.key(seed), 10)
    return {
        "latents": centred(key_list[0], (STEPS, S, C), 1.0, 6.0, ((0, 32), (1, 8)), jnp.float32),
        "residual": centred(key_list[1], (STEPS, S, D), 1.0, 6.0, ((0, 32),)),
        "timesteps": with_ends(jax.random.randint(key_list[2], (STEPS,), 0, 1000), jax.random.fold_in(key_list[2], 1), 0, 999).astype(jnp.int32),
        "step_sizes": jnp.clip(jnp.exp(math.log(0.06) - 1.3862944 * jax.random.uniform(key_list[3], (STEPS,), jnp.float32) ** block_levels(key_list[3], (STEPS,), ((0, 32),), -0.2, 0.2)), 0.015, 0.06),
        "embed_weight": draw_embed_weight(jax.random.fold_in(key_list[9], 71), 0),
        "mod_weight": centred(key_list[5], (3, FREQ, D), (FREQ // 4) ** -0.5, 0.75, ((2, 8),)),
        "up_weight": centred(key_list[6], (D, FF), D ** -0.5, 0.078125, ((0, 32), (1, 8))),
        "down_weight": centred(key_list[7], (FF, D), FF ** -0.5, 0.0625, ((0, 8), (1, 32))),
        "head_weight": centred(key_list[8], (D, C), D ** -0.5, 0.078125),
    }


def normalize(values):
    centre = values - lax.optimization_barrier(jnp.mean(values, axis=-1, keepdims=True))
    spread = lax.optimization_barrier(jnp.mean(centre * centre, axis=-1, keepdims=True))
    return centre * lax.rsqrt(spread + 1e-06)

def time_features(stamps, width):
    half = width // 2
    freqs = jnp.exp(-math.log(10000.0) * jnp.arange(half, dtype=jnp.float32) / half)
    angles = stamps.astype(jnp.float32)[:, None] * freqs[None, :]
    return jnp.concatenate([jnp.cos(angles), jnp.sin(angles)], axis=-1)

def reference(latents, residual, timesteps, step_sizes, embed_weight, mod_weight, up_weight, down_weight, head_weight):
    features = jax.nn.silu(time_features(timesteps, FREQ)).astype(jnp.bfloat16)

    def one_step(items):
        latent, stream, feature = items
        modulation = jnp.einsum('f,kfd->kd', feature.astype(jnp.float32), mod_weight.astype(jnp.float32))
        hidden = stream.astype(jnp.float32) + jnp.dot(latent.astype(jnp.bfloat16), embed_weight, preferred_element_type=jnp.float32)
        normed = (normalize(hidden) * (1.0 + modulation[1]) + modulation[0]).astype(jnp.bfloat16)
        preact = jnp.dot(normed, up_weight, preferred_element_type=jnp.float32)
        activated = jax.nn.gelu(preact, approximate=True).astype(jnp.bfloat16)
        width = FF // N_TENSOR
        mixed = jnp.zeros(hidden.shape, jnp.float32)
        for block in range(N_TENSOR):
            block_sum = jnp.dot(activated[:, block * width:(block + 1) * width], down_weight[block * width:(block + 1) * width], preferred_element_type=jnp.float32)
            rounded = lax.optimization_barrier(block_sum.astype(jnp.bfloat16))
            mixed = mixed + rounded.astype(jnp.float32)
        updated = hidden + modulation[2] * mixed
        return jnp.dot(normalize(updated).astype(jnp.bfloat16), head_weight, preferred_element_type=jnp.float32)
    drift = lax.map(one_step, (latents, residual, features))
    new_latents = latents[0][None] - jnp.cumsum(step_sizes[:, None, None] * drift, axis=0)
    return (drift, new_latents)
```

```python
import math

import jax
import jax.numpy as jnp
from jax import lax
from jax.sharding import PartitionSpec as P

STEPS = 32
CHUNKS = 4


def normalize(values):
    centre = values - jnp.mean(values, axis=-1, keepdims=True)
    spread = jnp.mean(centre * centre, axis=-1, keepdims=True)
    return centre * lax.rsqrt(spread + 1e-06)


def time_features(stamps, width):
    half = width // 2
    freqs = jnp.exp(-math.log(10000.0) * jnp.arange(half, dtype=jnp.float32) / half)
    angles = stamps.astype(jnp.float32)[:, None] * freqs[None, :]
    return jnp.concatenate([jnp.cos(angles), jnp.sin(angles)], axis=-1)


def running_sum(term):
    state = term
    hop = 1
    while hop < STEPS:
        pairs = [(i, i + hop) for i in range(STEPS - hop)]
        state = state + lax.ppermute(state, "tm", pairs)
        hop *= 2
    return state


def local(
    latents,
    residual,
    timesteps,
    step_sizes,
    embed_weight,
    mod_weight,
    up_weight,
    down_weight,
    head_weight,
):
    latent = latents[0]
    stream = residual[0]
    own_rows, channels = latent.shape
    width = stream.shape[1]
    depth = up_weight.shape[0]
    hidden_units = up_weight.shape[1]
    both = jnp.concatenate([up_weight, down_weight.T], axis=0)
    weights = lax.all_gather(both, "tm", axis=0)

    feature = jax.nn.silu(time_features(timesteps, mod_weight.shape[1])).astype(jnp.bfloat16)[0]
    piece_mod = jnp.einsum("f,kfd->kd", feature, mod_weight, preferred_element_type=jnp.float32)
    own = jnp.concatenate([piece_mod.reshape(-1), latent.reshape(-1)]).reshape(-1, 128)
    shared = lax.all_gather(own, "tensor", axis=0).reshape(8, -1)
    cut = piece_mod.size
    modulation = shared[:, :cut].reshape(8, 3, -1).transpose(1, 0, 2).reshape(3, width)
    all_latent = shared[:, cut:].reshape(8 * own_rows, channels)

    base = stream.astype(jnp.float32) + jnp.dot(
        all_latent.astype(jnp.bfloat16), embed_weight, preferred_element_type=jnp.float32
    )
    normed = (normalize(base) * (1.0 + modulation[1]) + modulation[0]).astype(jnp.bfloat16)

    row_start = lax.axis_index("tensor") * own_rows
    own_stream = lax.dynamic_slice_in_dim(stream, row_start, own_rows, 0)
    hidden = own_stream.astype(jnp.float32) + jnp.dot(
        latent.astype(jnp.bfloat16), embed_weight, preferred_element_type=jnp.float32
    )

    up = weights[:, :depth].reshape(width, hidden_units)
    preact = jnp.dot(normed, up, preferred_element_type=jnp.float32)
    activated = jax.nn.gelu(preact, approximate=True).astype(jnp.bfloat16)
    pieces = []
    per = STEPS // CHUNKS
    for c in range(CHUNKS):
        rows = weights[c * per : (c + 1) * per, depth:].reshape(per * depth, hidden_units)
        partial_sums = lax.dot_general(
            activated, rows, (((1,), (1,)), ((), ())), preferred_element_type=jnp.float32
        ).astype(jnp.bfloat16)
        pieces.append(lax.psum_scatter(partial_sums, "tensor", scatter_dimension=0, tiled=True))
    mixed = jnp.concatenate(pieces, axis=1).astype(jnp.float32)
    updated = hidden + modulation[2] * mixed
    drift = jnp.dot(
        normalize(updated).astype(jnp.bfloat16), head_weight, preferred_element_type=jnp.float32
    )
    first = (lax.axis_index("tm") == 0).astype(jnp.float32)
    new_latent = running_sum(first * latent - step_sizes[0] * drift)
    return (drift[None], new_latent[None])


def solution(mesh):
    in_specs = (
        P("tm", "tensor", None),
        P("tm", None, None),
        P("tm"),
        P("tm"),
        P(),
        P(None, None, "tensor"),
        P("tm", "tensor"),
        P("tensor", "tm"),
        P(),
    )
    out_specs = (P("tm", "tensor", None), P("tm", "tensor", None))
    return jax.shard_map(local, mesh=mesh, in_specs=in_specs, out_specs=out_specs, check_vma=False)
```

```python
import math

import jax
import jax.numpy as jnp
from jax import lax
from jax.sharding import PartitionSpec as P

NX, NZ, NY = 4, 8, 4
SPLIT = 384
CHUNKS = 4


def normalize(values):
    centre = values - jnp.mean(values, axis=-1, keepdims=True)
    spread = jnp.mean(centre * centre, axis=-1, keepdims=True)
    return centre * lax.rsqrt(spread + 1e-06)


def time_features(stamps, width):
    half = width // 2
    freqs = jnp.exp(-math.log(10000.0) * jnp.arange(half, dtype=jnp.float32) / half)
    angles = stamps.astype(jnp.float32)[:, None] * freqs[None, :]
    return jnp.concatenate([jnp.cos(angles), jnp.sin(angles)], axis=-1)


def send_x(value, hop):
    pairs = [(x * NZ + z, (x + hop) % NX * NZ + z) for x in range(NX) for z in range(NZ)]
    return lax.ppermute(value, "tm", pairs)


def send_z(value, hop):
    pairs = [(x * NZ + z, x * NZ + (z + hop) % NZ) for x in range(NX) for z in range(NZ)]
    return lax.ppermute(value, "tm", pairs)


def send_y(value, hop):
    pairs = [(y * 2 + c, (y + hop) % NY * 2 + c) for y in range(NY) for c in range(2)]
    return lax.ppermute(value, "tensor", pairs)


def send_core(value):
    pairs = [(y * 2 + c, y * 2 + 1 - c) for y in range(NY) for c in range(2)]
    return lax.ppermute(value, "tensor", pairs)


def turned(stack, place):
    count = stack.shape[0]
    start = lax.rem(count - place, count)
    return lax.dynamic_slice_in_dim(jnp.concatenate([stack, stack], axis=0), start, count, 0)


def gather_x(shard):
    half = shard.shape[0] // 2
    left, right = send_x(shard, 1), send_x(shard, -1)
    far = jnp.concatenate([send_x(left[:half], 1), send_x(right[half:], -1)], axis=0)
    return jnp.stack([shard, right, far, left])


def gather_z(shard):
    half = shard.shape[0] // 2
    left, right = [shard], [shard]
    for _ in range(3):
        left.append(send_z(left[-1], 1))
        right.append(send_z(right[-1], -1))
    far = jnp.concatenate([send_z(left[3][:half], 1), send_z(right[3][half:], -1)], axis=0)
    return [shard, right[1], right[2], right[3], far, left[3], left[2], left[1]]


def total_over_tensor(part, core, y):
    n = part.shape[-1]
    half = n // 2
    away = lax.dynamic_index_in_dim(part, 1 - core, 1, False)
    keep = lax.dynamic_index_in_dim(part, core, 1, False)
    both = keep.astype(jnp.float32) + send_core(away).astype(jnp.float32)

    def block(hop):
        return lax.dynamic_index_in_dim(both, lax.rem(y + hop, NY), 0, False)

    far = block(2).astype(jnp.bfloat16)
    low = send_y(far[:, :half], 1).astype(jnp.float32)
    high = send_y(far[:, half:], -1).astype(jnp.float32)
    ahead, behind = block(1), block(3)
    ahead = jnp.concatenate([ahead[:, :half] + low, ahead[:, half:]], axis=1)
    behind = jnp.concatenate([behind[:, :half], behind[:, half:] + high], axis=1)
    ahead = send_y(ahead.astype(jnp.bfloat16), 1).astype(jnp.float32)
    behind = send_y(behind.astype(jnp.bfloat16), -1).astype(jnp.float32)
    return block(0) + ahead + behind


def running_sum(term, x, z):
    before, after, far = send_x(term, 1), send_x(term, -1), send_x(term, 2)
    zero = jnp.zeros_like(term)
    whole = (
        jnp.where(x >= 1, before, zero)
        + jnp.where(x >= 2, far, zero)
        + jnp.where(x >= 3, after, zero)
    )
    mine = jnp.stack([whole, term])
    behind, ahead = send_z(mine, 1), send_z(mine, -1)
    triple = [(-1, behind), (0, mine), (1, ahead)]

    def share(pair, source, target):
        return pair[0] + jnp.where(source <= target, pair[1], jnp.zeros_like(term))

    def place(hop):
        return lax.rem(z + hop + 2 * NZ, NZ)

    up = sum(share(pair, place(d), place(3)) for d, pair in triple)
    down = sum(share(pair, place(d), place(-3)) for d, pair in triple if d != 1)
    total = share(mine, z, z) + share(behind, place(-1), z) + share(ahead, place(1), z)
    return total + send_z(up, 3) + send_z(down, -3)


def local(
    latents,
    residual,
    timesteps,
    step_sizes,
    embed_weight,
    mod_weight,
    up_weight,
    down_weight,
    head_weight,
):
    latent = latents[0]
    stream = residual[0]
    own_rows, channels = latent.shape
    width = stream.shape[1]
    depth, hidden_units = up_weight.shape
    place = lax.axis_index("tm")
    x, z = place // NZ, lax.rem(place, NZ)
    member = lax.axis_index("tensor")
    y, core = member // 2, lax.rem(member, 2)

    down = lax.all_gather(down_weight.T, "tm", axis=0)

    across = turned(gather_x(up_weight[:, :SPLIT]), x)
    along = turned(jnp.stack(gather_z(up_weight[:, SPLIT:])), z)

    up_a = jnp.zeros((NX, NZ, depth, SPLIT), jnp.bfloat16)
    for hop, block in enumerate(gather_z(across)):
        up_a = lax.dynamic_update_slice(
            up_a, block[:, None], (0, lax.rem(z + hop, NZ), 0, 0)
        )
    up_a = up_a.reshape(width, SPLIT)

    half = NZ // 2
    low, high = along[:half], along[half:]
    left_low, right_high = send_x(low, 1), send_x(high, -1)
    left_high, right_low = send_x(high, 1), send_x(low, -1)
    far_low, far_high = send_x(left_low, 1), send_x(right_high, -1)
    up_b = [(low, high), (right_low, right_high), (far_low, far_high), (left_low, left_high)]

    feature = jax.nn.silu(time_features(timesteps, mod_weight.shape[1])).astype(jnp.bfloat16)[0]
    piece_mod = jnp.einsum("f,kfd->kd", feature, mod_weight, preferred_element_type=jnp.float32)
    own = jnp.concatenate([piece_mod.reshape(-1), latent.reshape(-1)]).reshape(-1, 128)
    shared = lax.all_gather(own, "tensor", axis=0).reshape(8, -1)
    cut = piece_mod.size
    modulation = shared[:, :cut].reshape(8, 3, -1).transpose(1, 0, 2).reshape(3, width)
    all_latent = shared[:, cut:].reshape(8 * own_rows, channels)

    base = stream.astype(jnp.float32) + jnp.dot(
        all_latent.astype(jnp.bfloat16), embed_weight, preferred_element_type=jnp.float32
    )
    normed = (normalize(base) * (1.0 + modulation[1]) + modulation[0]).astype(jnp.bfloat16)

    own_stream = lax.dynamic_slice_in_dim(stream, member * own_rows, own_rows, 0)
    hidden = own_stream.astype(jnp.float32) + jnp.dot(
        latent.astype(jnp.bfloat16), embed_weight, preferred_element_type=jnp.float32
    )

    pre_a = jnp.dot(normed, up_a, preferred_element_type=jnp.float32)
    pre_b = jnp.zeros((normed.shape[0], hidden_units - SPLIT), jnp.float32)
    per = half * depth
    for hop, pair in enumerate(up_b):
        start = lax.rem(x + hop, NX) * (2 * per)
        for i, rows in enumerate(pair):
            columns = lax.dynamic_slice_in_dim(normed, start + i * per, per, 1)
            pre_b = pre_b + jnp.dot(
                columns, rows.reshape(per, -1), preferred_element_type=jnp.float32
            )
    act_a = jax.nn.gelu(pre_a, approximate=True).astype(jnp.bfloat16)
    act_b = jax.nn.gelu(pre_b, approximate=True).astype(jnp.bfloat16)
    activated = jnp.concatenate([act_a, act_b], axis=1)

    pieces = []
    count = down.shape[0] // CHUNKS
    for c in range(CHUNKS):
        rows = down[c * count : (c + 1) * count].reshape(count * depth, hidden_units)
        partial_sums = lax.dot_general(
            activated, rows, (((1,), (1,)), ((), ())), preferred_element_type=jnp.float32
        ).astype(jnp.bfloat16)
        part = partial_sums.reshape(NY, 2, own_rows, count * depth)
        pieces.append(total_over_tensor(part, core, y))
    mixed = jnp.concatenate(pieces, axis=1)
    updated = hidden + modulation[2] * mixed
    drift = jnp.dot(
        normalize(updated).astype(jnp.bfloat16), head_weight, preferred_element_type=jnp.float32
    )
    first = (place == 0).astype(jnp.float32)
    new_latent = running_sum(first * latent - step_sizes[0] * drift, x, z)
    return (drift[None], new_latent[None])


def solution(mesh):
    in_specs = (
        P("tm", "tensor", None),
        P("tm", None, None),
        P("tm"),
        P("tm"),
        P(),
        P(None, None, "tensor"),
        P("tm", "tensor"),
        P("tensor", "tm"),
        P(),
    )
    out_specs = (P("tm", "tensor", None), P("tm", "tensor", None))
    return jax.shard_map(local, mesh=mesh, in_specs=in_specs, out_specs=out_specs, check_vma=False)
```

```python
import math

import jax
import jax.numpy as jnp
from jax import lax
from jax.experimental import pallas as pl
from jax.experimental.pallas import tpu as pltpu
from jax.sharding import PartitionSpec as P

NX, NZ, NY = 4, 8, 4
SPLIT = 64
CHUNKS = (16, 16)


def normalize(values):
    centre = values - jnp.mean(values, axis=-1, keepdims=True)
    spread = jnp.mean(centre * centre, axis=-1, keepdims=True)
    return centre * lax.rsqrt(spread + 1e-06)


def time_features(stamps, width):
    half = width // 2
    freqs = jnp.exp(-math.log(10000.0) * jnp.arange(half, dtype=jnp.float32) / half)
    angles = stamps.astype(jnp.float32)[:, None] * freqs[None, :]
    return jnp.concatenate([jnp.cos(angles), jnp.sin(angles)], axis=-1)


def send_x(value, hop):
    pairs = [(x * NZ + z, (x + hop) % NX * NZ + z) for x in range(NX) for z in range(NZ)]
    return lax.ppermute(value, "tm", pairs)


def send_z(value, hop):
    pairs = [(x * NZ + z, x * NZ + (z + hop) % NZ) for x in range(NX) for z in range(NZ)]
    return lax.ppermute(value, "tm", pairs)


def send_y(value, hop):
    pairs = [(y * 2 + c, (y + hop) % NY * 2 + c) for y in range(NY) for c in range(2)]
    return lax.ppermute(value, "tensor", pairs)


def send_core(value):
    pairs = [(y * 2 + c, y * 2 + 1 - c) for y in range(NY) for c in range(2)]
    return lax.ppermute(value, "tensor", pairs)


def after(values, done):
    count = len(values)
    return lax.optimization_barrier((*values, *done))[:count]


def normed_kernel(latent_ref, embed_ref, stream_ref, gain_ref, shift_ref, out_ref):
    values = stream_ref[...].astype(jnp.float32) + jnp.dot(
        latent_ref[...], embed_ref[...], preferred_element_type=jnp.float32
    )
    scaled = normalize(values) * gain_ref[...] + shift_ref[...]
    out_ref[...] = scaled.astype(out_ref.dtype)


def normed_rows(latent, embed, stream, gain, shift):
    rows, width = stream.shape
    channels = latent.shape[1]
    per = 80
    return pl.pallas_call(
        normed_kernel,
        grid=(rows // per,),
        in_specs=[
            pl.BlockSpec((per, channels), lambda i: (i, 0)),
            pl.BlockSpec((channels, width), lambda i: (0, 0)),
            pl.BlockSpec((per, width), lambda i: (i, 0)),
            pl.BlockSpec((1, width), lambda i: (0, 0)),
            pl.BlockSpec((1, width), lambda i: (0, 0)),
        ],
        out_specs=pl.BlockSpec((per, width), lambda i: (i, 0)),
        out_shape=jax.ShapeDtypeStruct((rows, width), jnp.bfloat16),
        compiler_params=pltpu.CompilerParams(vmem_limit_bytes=24 * 2**20),
        cost_estimate=pl.CostEstimate(
            flops=rows * width * (2 * channels + 16),
            transcendentals=rows,
            bytes_accessed=4 * rows * width,
        ),
        name="normed_rows",
    )(latent, embed, stream, gain, shift)


def placed_kernel(spots, *refs):
    pieces, (out_ref, zeros, sem) = refs[:-3], refs[-3:]
    x, z = spots[0], spots[1]
    depth = out_ref.shape[0] // (NX * NZ)
    late = depth - SPLIT
    half_late = late // 2
    copies = []

    def put(source, hop_x, hop_z, start, rows):
        place = lax.rem(x + hop_x, NX) * NZ + lax.rem(z + hop_z, NZ)
        spot = pl.ds(pl.multiple_of(place * depth + start, 16), rows)
        copy = pltpu.make_async_copy(source, out_ref.at[spot, :], sem.at[len(copies)])
        copy.start()
        copies.append(copy)

    def take(piece, row, hop_x, hop_z, start, rows):
        put(pieces[piece].at[pl.ds(row, rows), :], hop_x, hop_z, start, rows)

    own, left3, right3, left4, right4, left5, right5 = range(7)
    near, near_right, near_left, near_low, near_high = range(7, 12)
    rest, rest_right, rest_left = range(12, 15)
    hops = ((own, 0), (right3, 1), (right4, 2), (right5, 3), (left5, 5), (left4, 6), (left3, 7))
    zeros[...] = jnp.zeros_like(zeros)
    for hop_x in range(NX):
        for piece, hop in hops:
            take(piece, hop_x * SPLIT, hop_x, hop, 0, SPLIT)
        put(zeros.at[pl.ds(0, SPLIT), :], hop_x, NZ // 2, 0, SPLIT)
        for i, hop in enumerate(NEAR):
            if hop_x == 2:
                piece, row = (near_low, i) if i < 3 else (near_high, i - 3)
            else:
                piece, row = (near, near_right, None, near_left)[hop_x], i
            take(piece, row * late, hop_x, hop, SPLIT, late)
        for i, hop in enumerate(REST):
            if hop_x == 2:
                put(zeros.at[pl.ds(0, late), :], hop_x, hop, SPLIT, late)
            else:
                piece = (rest, rest_right, None, rest_left)[hop_x]
                take(piece, i * late, hop_x, hop, SPLIT, late)
    for copy in copies:
        copy.wait()


NEAR = (0, 1, 2, 6, 7)
REST = (3, 4, 5)
COPIES = NX * (NZ + len(NEAR) + len(REST))


def placed(pieces, width):
    columns = pieces[0].shape[1]
    late = width // (NX * NZ) - SPLIT
    place = lax.axis_index("tm")
    spots = jnp.stack([place // NZ, lax.rem(place, NZ)]).astype(jnp.int32)
    return pl.pallas_call(
        placed_kernel,
        grid_spec=pltpu.PrefetchScalarGridSpec(
            num_scalar_prefetch=1,
            grid=(1,),
            in_specs=[pl.BlockSpec(memory_space=pl.ANY)] * len(pieces),
            out_specs=pl.BlockSpec((width, columns), lambda i, spots: (0, 0)),
            scratch_shapes=[
                pltpu.VMEM((max(SPLIT, late), columns), jnp.bfloat16),
                pltpu.SemaphoreType.DMA((COPIES,)),
            ],
        ),
        out_shape=jax.ShapeDtypeStruct((width, columns), jnp.bfloat16),
        cost_estimate=pl.CostEstimate(
            flops=0, transcendentals=0, bytes_accessed=4 * width * columns
        ),
        compiler_params=pltpu.CompilerParams(vmem_limit_bytes=32 * 2**20),
        name="placed",
    )(spots, *pieces)


def moved(sends, *others):
    arrived = [move(value, hop) for value, move, hop in sends]
    return lax.optimization_barrier((*arrived, *others))


def total_over_cores(part, core):
    away = lax.dynamic_index_in_dim(part, 1 - core, 1, False)
    keep = lax.dynamic_index_in_dim(part, core, 1, False)
    return keep.astype(jnp.float32) + send_core(away).astype(jnp.float32)


def total_over_chips(both, y):
    half = both.shape[-1] // 2

    def block(hop):
        return lax.dynamic_index_in_dim(both, lax.rem(y + hop, NY), 0, False)

    far = block(2).astype(jnp.bfloat16)
    low = send_y(far[:, :half], 1).astype(jnp.float32)
    high = send_y(far[:, half:], -1).astype(jnp.float32)
    ahead, behind = block(1), block(3)
    ahead = jnp.concatenate([ahead[:, :half] + low, ahead[:, half:]], axis=1)
    behind = jnp.concatenate([behind[:, :half], behind[:, half:] + high], axis=1)
    ahead = send_y(ahead.astype(jnp.bfloat16), 1).astype(jnp.float32)
    behind = send_y(behind.astype(jnp.bfloat16), -1).astype(jnp.float32)
    return block(0) + ahead + behind


def running_sum(term, x, z):
    before, after, far = send_x(term, 1), send_x(term, -1), send_x(term, 2)
    zero = jnp.zeros_like(term)
    whole = (
        jnp.where(x >= 1, before, zero)
        + jnp.where(x >= 2, far, zero)
        + jnp.where(x >= 3, after, zero)
    )
    mine = jnp.stack([whole, term])
    behind, ahead = send_z(mine, 1), send_z(mine, -1)
    triple = [(-1, behind), (0, mine), (1, ahead)]

    def share(pair, source, target):
        return pair[0] + jnp.where(source <= target, pair[1], jnp.zeros_like(term))

    def place(hop):
        return lax.rem(z + hop + 2 * NZ, NZ)

    up = sum(share(pair, place(d), place(3)) for d, pair in triple)
    down = sum(share(pair, place(d), place(-3)) for d, pair in triple if d != 1)
    total = share(mine, z, z) + share(behind, place(-1), z) + share(ahead, place(1), z)
    return total + send_z(up, 3) + send_z(down, -3)


def local(
    latents,
    residual,
    timesteps,
    step_sizes,
    embed_weight,
    mod_weight,
    up_weight,
    down_weight,
    head_weight,
):
    latent = latents[0]
    stream = residual[0]
    own_rows, channels = latent.shape
    width = stream.shape[1]
    depth, hidden_units = up_weight.shape
    place = lax.axis_index("tm")
    x, z = place // NZ, lax.rem(place, NZ)
    member = lax.axis_index("tensor")
    y, core = member // 2, lax.rem(member, 2)

    down = lax.all_gather(down_weight.T, "tm", axis=0)

    late = depth - SPLIT
    first, second = up_weight[:SPLIT], up_weight[SPLIT:]

    feature = jax.nn.silu(time_features(timesteps, mod_weight.shape[1])).astype(jnp.bfloat16)[0]
    piece_mod = jnp.einsum("f,kfd->kd", feature, mod_weight, preferred_element_type=jnp.float32)
    own = jnp.concatenate([piece_mod.reshape(-1), latent.reshape(-1)]).reshape(-1, 128)

    a_left, a_right, b_left1, b_right1, own, first, second = moved(
        [(first, send_x, 1), (first, send_x, -1), (second, send_z, 1), (second, send_z, -1)],
        own,
        first,
        second,
    )
    a_low, a_high, b_left2, b_right2, own = moved(
        [
            (a_left[: SPLIT // 2], send_x, 1),
            (a_right[SPLIT // 2 :], send_x, -1),
            (b_left1, send_z, 1),
            (b_right1, send_z, -1),
        ],
        own,
    )
    block = jnp.concatenate([first, a_right, a_low, a_high, a_left], axis=0)
    near = jnp.concatenate([second, b_right1, b_right2, b_left2, b_left1], axis=0)
    left3 = jnp.concatenate([block, b_left2], axis=0)
    right3 = jnp.concatenate([block, b_right2], axis=0)
    block, near, left3, right3 = lax.optimization_barrier((block, near, left3, right3))
    shared = lax.all_gather(own, "tensor", axis=0)
    left3, right3, near_left, near_right, shared = moved(
        [
            (left3, send_z, 1),
            (right3, send_z, -1),
            (near, send_x, 1),
            (near, send_x, -1),
        ],
        shared,
    )
    shared = shared.reshape(8, -1)
    cut = piece_mod.size
    modulation = shared[:, :cut].reshape(8, 3, -1).transpose(1, 0, 2).reshape(3, width)
    all_latent = shared[:, cut:].reshape(8 * own_rows, channels).astype(jnp.bfloat16)
    gain, shift = 1.0 + modulation[1][None], modulation[0][None]
    normed = normed_rows(all_latent, embed_weight, stream, gain, shift)
    span = NX * SPLIT
    left4, right4, near_low, near_high, normed = moved(
        [
            (left3[: span + late // 2], send_z, 1),
            (
                jnp.concatenate([right3[:span], right3[span + late // 2 :]], axis=0),
                send_z,
                -1,
            ),
            (near_left[: 3 * late], send_x, 1),
            (near_right[3 * late :], send_x, -1),
        ],
        normed,
    )
    rest = jnp.concatenate([right3[span:], left4[span:], right4[span:], left3[span:]], axis=0)
    left5, right5, rest_left, rest_right = moved(
        [
            (left4[:span], send_z, 1),
            (right4[:span], send_z, -1),
            (rest, send_x, 1),
            (rest, send_x, -1),
        ],
    )

    def halves(rows, start):
        cut_rows = rows.reshape(3, late, hidden_units)[:, start : start + late // 2]
        return cut_rows.reshape(3 * late // 2, hidden_units)

    pieces = [block, left3, right3, left4, right4, left5, right5]
    pieces += [near, near_right, near_left, near_low, near_high]
    pieces += [rest, rest_right, rest_left]
    preact = jnp.dot(normed, placed(pieces, width), preferred_element_type=jnp.float32)

    def columns(hop_x, hop_z, start, count):
        shard = lax.rem(x + hop_x, NX) * NZ + lax.rem(z + hop_z, NZ)
        return lax.dynamic_slice_in_dim(normed, shard * depth + start, count, 1)

    missing = [columns(hop_x, NZ // 2, 0, SPLIT) for hop_x in range(NX)]
    for start in (SPLIT, SPLIT + late // 2):
        missing += [columns(2, hop, start, late // 2) for hop in REST]
    missing = jnp.concatenate(missing, axis=1)
    left6, right6, rest_low, rest_high, preact, missing = moved(
        [
            (left5[: span // 2], send_z, 1),
            (right5[span // 2 :], send_z, -1),
            (halves(rest_left, 0), send_x, 1),
            (halves(rest_right, late // 2), send_x, -1),
        ],
        preact,
        missing,
    )
    last = jnp.concatenate([left6, right6, rest_low, rest_high], axis=0)
    preact = preact + jnp.dot(missing, last, preferred_element_type=jnp.float32)
    activated = jax.nn.gelu(preact, approximate=True).astype(jnp.bfloat16)

    own_stream = lax.dynamic_slice_in_dim(stream, member * own_rows, own_rows, 0)
    hidden = own_stream.astype(jnp.float32) + jnp.dot(
        latent.astype(jnp.bfloat16), embed_weight, preferred_element_type=jnp.float32
    )

    totals = []
    start = 0
    for count in CHUNKS:
        rows = down[start : start + count].reshape(count * depth, hidden_units)
        start += count
        partial_sums = lax.dot_general(
            activated, rows, (((1,), (1,)), ((), ())), preferred_element_type=jnp.float32
        ).astype(jnp.bfloat16)
        part = partial_sums.reshape(NY, 2, own_rows, count * depth)
        both = total_over_cores(part, core)
        activated, both = lax.optimization_barrier((activated, both))
        totals.append(total_over_chips(both, y))
    mixed = jnp.concatenate(totals, axis=1)
    updated = hidden + modulation[2] * mixed
    drift = jnp.dot(
        normalize(updated).astype(jnp.bfloat16), head_weight, preferred_element_type=jnp.float32
    )
    first = (place == 0).astype(jnp.float32)
    new_latent = running_sum(first * latent - step_sizes[0] * drift, x, z)
    return (drift[None], new_latent[None])


def solution(mesh):
    in_specs = (
        P("tm", "tensor", None),
        P("tm", None, None),
        P("tm"),
        P("tm"),
        P(),
        P(None, None, "tensor"),
        P("tm", "tensor"),
        P("tensor", "tm"),
        P(),
    )
    out_specs = (P("tm", "tensor", None), P("tm", "tensor", None))
    return jax.shard_map(local, mesh=mesh, in_specs=in_specs, out_specs=out_specs, check_vma=False)
```

```python
import math

import jax
import jax.numpy as jnp
from jax import lax
from jax.experimental import pallas as pl
from jax.experimental.pallas import tpu as pltpu
from jax.sharding import PartitionSpec as P

NX, NZ, NY = 4, 8, 4
SPLIT = 64
CHUNKS = (16, 16)


def normalize(values):
    centre = values - jnp.mean(values, axis=-1, keepdims=True)
    spread = jnp.mean(centre * centre, axis=-1, keepdims=True)
    return centre * lax.rsqrt(spread + 1e-06)


def time_features(stamps, width):
    half = width // 2
    freqs = jnp.exp(-math.log(10000.0) * jnp.arange(half, dtype=jnp.float32) / half)
    angles = stamps.astype(jnp.float32)[:, None] * freqs[None, :]
    return jnp.concatenate([jnp.cos(angles), jnp.sin(angles)], axis=-1)


def send_x(value, hop):
    pairs = [(x * NZ + z, (x + hop) % NX * NZ + z) for x in range(NX) for z in range(NZ)]
    return lax.ppermute(value, "tm", pairs)


def send_z(value, hop):
    pairs = [(x * NZ + z, x * NZ + (z + hop) % NZ) for x in range(NX) for z in range(NZ)]
    return lax.ppermute(value, "tm", pairs)


def send_y(value, hop):
    pairs = [(y * 2 + c, (y + hop) % NY * 2 + c) for y in range(NY) for c in range(2)]
    return lax.ppermute(value, "tensor", pairs)


def send_core(value):
    pairs = [(y * 2 + c, y * 2 + 1 - c) for y in range(NY) for c in range(2)]
    return lax.ppermute(value, "tensor", pairs)


def after(values, done):
    count = len(values)
    return lax.optimization_barrier((*values, *done))[:count]


def normed_kernel(latent_ref, embed_ref, stream_ref, gain_ref, shift_ref, out_ref):
    values = stream_ref[...].astype(jnp.float32) + jnp.dot(
        latent_ref[...], embed_ref[...], preferred_element_type=jnp.float32
    )
    scaled = normalize(values) * gain_ref[...] + shift_ref[...]
    out_ref[...] = scaled.astype(out_ref.dtype)


def normed_rows(latent, embed, stream, gain, shift):
    rows, width = stream.shape
    channels = latent.shape[1]
    per = 80
    return pl.pallas_call(
        normed_kernel,
        grid=(rows // per,),
        in_specs=[
            pl.BlockSpec((per, channels), lambda i: (i, 0)),
            pl.BlockSpec((channels, width), lambda i: (0, 0)),
            pl.BlockSpec((per, width), lambda i: (i, 0)),
            pl.BlockSpec((1, width), lambda i: (0, 0)),
            pl.BlockSpec((1, width), lambda i: (0, 0)),
        ],
        out_specs=pl.BlockSpec((per, width), lambda i: (i, 0)),
        out_shape=jax.ShapeDtypeStruct((rows, width), jnp.bfloat16),
        compiler_params=pltpu.CompilerParams(vmem_limit_bytes=24 * 2**20),
        cost_estimate=pl.CostEstimate(
            flops=rows * width * (2 * channels + 16),
            transcendentals=rows,
            bytes_accessed=4 * rows * width,
        ),
        name="normed_rows",
    )(latent, embed, stream, gain, shift)


def placed_kernel(spots, *refs):
    pieces, (out_ref, zeros, sem) = refs[:-3], refs[-3:]
    x, z = spots[0], spots[1]
    depth = out_ref.shape[0] // (NX * NZ)
    late = depth - SPLIT
    half_late = late // 2
    copies = []

    def put(source, hop_x, hop_z, start, rows):
        place = lax.rem(x + hop_x, NX) * NZ + lax.rem(z + hop_z, NZ)
        spot = pl.ds(pl.multiple_of(place * depth + start, 16), rows)
        copy = pltpu.make_async_copy(source, out_ref.at[spot, :], sem.at[len(copies)])
        copy.start()
        copies.append(copy)

    def take(piece, row, hop_x, hop_z, start, rows):
        put(pieces[piece].at[pl.ds(row, rows), :], hop_x, hop_z, start, rows)

    own, left3, right3, left4, right4, left5, right5 = range(7)
    near, near_right, near_left, near_low, near_high = range(7, 12)
    rest, rest_right, rest_left = range(12, 15)
    hops = ((own, 0), (right3, 1), (right4, 2), (right5, 3), (left5, 5), (left4, 6), (left3, 7))
    zeros[...] = jnp.zeros_like(zeros)
    for hop_x in range(NX):
        for piece, hop in hops:
            take(piece, hop_x * SPLIT, hop_x, hop, 0, SPLIT)
        put(zeros.at[pl.ds(0, SPLIT), :], hop_x, NZ // 2, 0, SPLIT)
        for i, hop in enumerate(NEAR):
            if hop_x == 2:
                piece, row = (near_low, i) if i < 3 else (near_high, i - 3)
            else:
                piece, row = (near, near_right, None, near_left)[hop_x], i
            take(piece, row * late, hop_x, hop, SPLIT, late)
        for i, hop in enumerate(REST):
            if hop_x == 2:
                put(zeros.at[pl.ds(0, late), :], hop_x, hop, SPLIT, late)
            else:
                piece = (rest, rest_right, None, rest_left)[hop_x]
                take(piece, i * late, hop_x, hop, SPLIT, late)
    for copy in copies:
        copy.wait()


NEAR = (0, 1, 2, 6, 7)
REST = (3, 4, 5)
COPIES = NX * (NZ + len(NEAR) + len(REST))


def placed(pieces, width):
    columns = pieces[0].shape[1]
    late = width // (NX * NZ) - SPLIT
    place = lax.axis_index("tm")
    spots = jnp.stack([place // NZ, lax.rem(place, NZ)]).astype(jnp.int32)
    return pl.pallas_call(
        placed_kernel,
        grid_spec=pltpu.PrefetchScalarGridSpec(
            num_scalar_prefetch=1,
            grid=(1,),
            in_specs=[pl.BlockSpec(memory_space=pl.ANY)] * len(pieces),
            out_specs=pl.BlockSpec(memory_space=pltpu.VMEM),
            scratch_shapes=[
                pltpu.VMEM((max(SPLIT, late), columns), jnp.bfloat16),
                pltpu.SemaphoreType.DMA((COPIES,)),
            ],
        ),
        out_shape=jax.ShapeDtypeStruct((width, columns), jnp.bfloat16),
        cost_estimate=pl.CostEstimate(
            flops=0, transcendentals=0, bytes_accessed=4 * width * columns
        ),
        compiler_params=pltpu.CompilerParams(vmem_limit_bytes=32 * 2**20),
        name="placed",
    )(spots, *pieces)


def moved(sends, *others):
    arrived = [move(value, hop) for value, move, hop in sends]
    return lax.optimization_barrier((*arrived, *others))


def spread_kernel(core_ref, act_ref, down_ref, keep_ref, away_ref):
    full = lax.dot_general(
        act_ref[...],
        down_ref[...],
        (((1,), (1,)), ((), ())),
        preferred_element_type=jnp.float32,
    )
    even_mine = core_ref[0] == 0
    rows = keep_ref.shape[1]
    for y in range(NY):
        even = full[2 * y * rows : (2 * y + 1) * rows]
        odd = full[(2 * y + 1) * rows : (2 * y + 2) * rows]
        keep_ref[y] = jnp.where(even_mine, even, odd).astype(keep_ref.dtype)
        away_ref[y] = jnp.where(even_mine, odd, even).astype(away_ref.dtype)


def spread(activated, down, core, start, count):
    rows, units = activated.shape
    own = rows // (2 * NY)
    per = 640
    shape = jax.ShapeDtypeStruct((NY, own, count), jnp.bfloat16)
    block = pl.BlockSpec((NY, own, per), lambda i, core: (0, 0, i))
    return pl.pallas_call(
        spread_kernel,
        grid_spec=pltpu.PrefetchScalarGridSpec(
            num_scalar_prefetch=1,
            grid=(count // per,),
            in_specs=[
                pl.BlockSpec((rows, units), lambda i, core: (0, 0)),
                pl.BlockSpec((per, units), lambda i, core: (start // per + i, 0)),
            ],
            out_specs=[block, block],
        ),
        out_shape=(shape, shape),
        compiler_params=pltpu.CompilerParams(vmem_limit_bytes=24 * 2**20),
        cost_estimate=pl.CostEstimate(
            flops=2 * rows * units * count,
            transcendentals=0,
            bytes_accessed=2 * (rows * units + units * count + rows * count),
        ),
        name="spread",
    )(core[None].astype(jnp.int32), activated, down)


def total_over_chips(both, y):
    half = both.shape[-1] // 2

    def block(hop):
        return lax.dynamic_index_in_dim(both, lax.rem(y + hop, NY), 0, False)

    far = block(2).astype(jnp.bfloat16)
    low = send_y(far[:, :half], 1).astype(jnp.float32)
    high = send_y(far[:, half:], -1).astype(jnp.float32)
    ahead, behind = block(1), block(3)
    ahead = jnp.concatenate([ahead[:, :half] + low, ahead[:, half:]], axis=1)
    behind = jnp.concatenate([behind[:, :half], behind[:, half:] + high], axis=1)
    ahead = send_y(ahead.astype(jnp.bfloat16), 1).astype(jnp.float32)
    behind = send_y(behind.astype(jnp.bfloat16), -1).astype(jnp.float32)
    return block(0) + ahead + behind


def running_sum(term, x, z):
    before, after, far = send_x(term, 1), send_x(term, -1), send_x(term, 2)
    zero = jnp.zeros_like(term)
    whole = (
        jnp.where(x >= 1, before, zero)
        + jnp.where(x >= 2, far, zero)
        + jnp.where(x >= 3, after, zero)
    )
    mine = jnp.stack([whole, term])
    behind, ahead = send_z(mine, 1), send_z(mine, -1)
    triple = [(-1, behind), (0, mine), (1, ahead)]

    def share(pair, source, target):
        return pair[0] + jnp.where(source <= target, pair[1], jnp.zeros_like(term))

    def place(hop):
        return lax.rem(z + hop + 2 * NZ, NZ)

    up = sum(share(pair, place(d), place(3)) for d, pair in triple)
    down = sum(share(pair, place(d), place(-3)) for d, pair in triple if d != 1)
    total = share(mine, z, z) + share(behind, place(-1), z) + share(ahead, place(1), z)
    return total + send_z(up, 3) + send_z(down, -3)


def local(
    latents,
    residual,
    timesteps,
    step_sizes,
    embed_weight,
    mod_weight,
    up_weight,
    down_weight,
    head_weight,
):
    latent = latents[0]
    stream = residual[0]
    own_rows, channels = latent.shape
    width = stream.shape[1]
    depth, hidden_units = up_weight.shape
    place = lax.axis_index("tm")
    x, z = place // NZ, lax.rem(place, NZ)
    member = lax.axis_index("tensor")
    y, core = member // 2, lax.rem(member, 2)

    down = lax.all_gather(down_weight.T, "tm", axis=0)

    late = depth - SPLIT
    first, second = up_weight[:SPLIT], up_weight[SPLIT:]

    feature = jax.nn.silu(time_features(timesteps, mod_weight.shape[1])).astype(jnp.bfloat16)[0]
    piece_mod = jnp.einsum("f,kfd->kd", feature, mod_weight, preferred_element_type=jnp.float32)
    own = jnp.concatenate([piece_mod.reshape(-1), latent.reshape(-1)]).reshape(-1, 128)

    a_left, a_right, b_left1, b_right1, own, first, second = moved(
        [(first, send_x, 1), (first, send_x, -1), (second, send_z, 1), (second, send_z, -1)],
        own,
        first,
        second,
    )
    a_low, a_high, b_left2, b_right2, own = moved(
        [
            (a_left[: SPLIT // 2], send_x, 1),
            (a_right[SPLIT // 2 :], send_x, -1),
            (b_left1, send_z, 1),
            (b_right1, send_z, -1),
        ],
        own,
    )
    block = jnp.concatenate([first, a_right, a_low, a_high, a_left], axis=0)
    near = jnp.concatenate([second, b_right1, b_right2, b_left2, b_left1], axis=0)
    left3 = jnp.concatenate([block, b_left2], axis=0)
    right3 = jnp.concatenate([block, b_right2], axis=0)
    block, near, left3, right3 = lax.optimization_barrier((block, near, left3, right3))
    shared = lax.all_gather(own, "tensor", axis=0)
    left3, right3, near_left, near_right, shared = moved(
        [
            (left3, send_z, 1),
            (right3, send_z, -1),
            (near, send_x, 1),
            (near, send_x, -1),
        ],
        shared,
    )
    shared = shared.reshape(8, -1)
    cut = piece_mod.size
    modulation = shared[:, :cut].reshape(8, 3, -1).transpose(1, 0, 2).reshape(3, width)
    all_latent = shared[:, cut:].reshape(8 * own_rows, channels).astype(jnp.bfloat16)
    gain, shift = 1.0 + modulation[1][None], modulation[0][None]
    normed = normed_rows(all_latent, embed_weight, stream, gain, shift)
    span = NX * SPLIT
    left4, right4, near_low, near_high, normed = moved(
        [
            (left3[: span + late // 2], send_z, 1),
            (
                jnp.concatenate([right3[:span], right3[span + late // 2 :]], axis=0),
                send_z,
                -1,
            ),
            (near_left[: 3 * late], send_x, 1),
            (near_right[3 * late :], send_x, -1),
        ],
        normed,
    )
    rest = jnp.concatenate([right3[span:], left4[span:], right4[span:], left3[span:]], axis=0)
    left5, right5, rest_left, rest_right = moved(
        [
            (left4[:span], send_z, 1),
            (right4[:span], send_z, -1),
            (rest, send_x, 1),
            (rest, send_x, -1),
        ],
    )

    def halves(rows, start):
        cut_rows = rows.reshape(3, late, hidden_units)[:, start : start + late // 2]
        return cut_rows.reshape(3 * late // 2, hidden_units)

    pieces = [block, left3, right3, left4, right4, left5, right5]
    pieces += [near, near_right, near_left, near_low, near_high]
    pieces += [rest, rest_right, rest_left]
    preact = jnp.dot(normed, placed(pieces, width), preferred_element_type=jnp.float32)

    def columns(hop_x, hop_z, start, count):
        shard = lax.rem(x + hop_x, NX) * NZ + lax.rem(z + hop_z, NZ)
        return lax.dynamic_slice_in_dim(normed, shard * depth + start, count, 1)

    missing = [columns(hop_x, NZ // 2, 0, SPLIT) for hop_x in range(NX)]
    for start in (SPLIT, SPLIT + late // 2):
        missing += [columns(2, hop, start, late // 2) for hop in REST]
    missing = jnp.concatenate(missing, axis=1)
    left6, right6, rest_low, rest_high, preact, missing = moved(
        [
            (left5[: span // 2], send_z, 1),
            (right5[span // 2 :], send_z, -1),
            (halves(rest_left, 0), send_x, 1),
            (halves(rest_right, late // 2), send_x, -1),
        ],
        preact,
        missing,
    )
    last = jnp.concatenate([left6, right6, rest_low, rest_high], axis=0)
    preact = preact + jnp.dot(missing, last, preferred_element_type=jnp.float32)
    activated = jax.nn.gelu(preact, approximate=True).astype(jnp.bfloat16)

    own_stream = lax.dynamic_slice_in_dim(stream, member * own_rows, own_rows, 0)
    hidden = own_stream.astype(jnp.float32) + jnp.dot(
        latent.astype(jnp.bfloat16), embed_weight, preferred_element_type=jnp.float32
    )

    totals = []
    start = 0
    down = down.reshape(width, hidden_units)
    down = pltpu.with_memory_space_constraint(down, pltpu.HBM)
    for shards in CHUNKS:
        count = shards * depth
        keep, away = spread(activated, down, core, start, count)
        start += count
        both = keep.astype(jnp.float32) + send_core(away).astype(jnp.float32)
        totals.append(total_over_chips(both, y))
    mixed = jnp.concatenate(totals, axis=1)
    updated = hidden + modulation[2] * mixed
    drift = jnp.dot(
        normalize(updated).astype(jnp.bfloat16), head_weight, preferred_element_type=jnp.float32
    )
    first = (place == 0).astype(jnp.float32)
    new_latent = running_sum(first * latent - step_sizes[0] * drift, x, z)
    return (drift[None], new_latent[None])


def solution(mesh):
    in_specs = (
        P("tm", "tensor", None),
        P("tm", None, None),
        P("tm"),
        P("tm"),
        P(),
        P(None, None, "tensor"),
        P("tm", "tensor"),
        P("tensor", "tm"),
        P(),
    )
    out_specs = (P("tm", "tensor", None), P("tm", "tensor", None))
    return jax.shard_map(local, mesh=mesh, in_specs=in_specs, out_specs=out_specs, check_vma=False)
```

```python
import math

import jax
import jax.numpy as jnp
from jax import lax
from jax.experimental import pallas as pl
from jax.experimental.pallas import tpu as pltpu
from jax.sharding import PartitionSpec as P

NX, NZ, NY = 4, 8, 4
SPLIT = 64
CHUNKS = (16, 16)


def normalize(values):
    centre = values - jnp.mean(values, axis=-1, keepdims=True)
    spread = jnp.mean(centre * centre, axis=-1, keepdims=True)
    return centre * lax.rsqrt(spread + 1e-06)


def time_features(stamps, width):
    half = width // 2
    freqs = jnp.exp(-math.log(10000.0) * jnp.arange(half, dtype=jnp.float32) / half)
    angles = stamps.astype(jnp.float32)[:, None] * freqs[None, :]
    return jnp.concatenate([jnp.cos(angles), jnp.sin(angles)], axis=-1)


def send_x(value, hop):
    pairs = [(x * NZ + z, (x + hop) % NX * NZ + z) for x in range(NX) for z in range(NZ)]
    return lax.ppermute(value, "tm", pairs)


def send_z(value, hop):
    pairs = [(x * NZ + z, x * NZ + (z + hop) % NZ) for x in range(NX) for z in range(NZ)]
    return lax.ppermute(value, "tm", pairs)


def send_y(value, hop):
    pairs = [(y * 2 + c, (y + hop) % NY * 2 + c) for y in range(NY) for c in range(2)]
    return lax.ppermute(value, "tensor", pairs)


def send_core(value):
    pairs = [(y * 2 + c, y * 2 + 1 - c) for y in range(NY) for c in range(2)]
    return lax.ppermute(value, "tensor", pairs)


def after(values, done):
    count = len(values)
    return lax.optimization_barrier((*values, *done))[:count]


def normed_kernel(latent_ref, embed_ref, stream_ref, gain_ref, shift_ref, out_ref):
    values = stream_ref[...].astype(jnp.float32) + jnp.dot(
        latent_ref[...], embed_ref[...], preferred_element_type=jnp.float32
    )
    scaled = normalize(values) * gain_ref[...] + shift_ref[...]
    out_ref[...] = scaled.astype(out_ref.dtype)


def normed_rows(latent, embed, stream, gain, shift):
    rows, width = stream.shape
    channels = latent.shape[1]
    per = 80
    return pl.pallas_call(
        normed_kernel,
        grid=(rows // per,),
        in_specs=[
            pl.BlockSpec((per, channels), lambda i: (i, 0)),
            pl.BlockSpec((channels, width), lambda i: (0, 0)),
            pl.BlockSpec((per, width), lambda i: (i, 0)),
            pl.BlockSpec((1, width), lambda i: (0, 0)),
            pl.BlockSpec((1, width), lambda i: (0, 0)),
        ],
        out_specs=pl.BlockSpec((per, width), lambda i: (i, 0)),
        out_shape=jax.ShapeDtypeStruct((rows, width), jnp.bfloat16),
        compiler_params=pltpu.CompilerParams(vmem_limit_bytes=24 * 2**20),
        cost_estimate=pl.CostEstimate(
            flops=rows * width * (2 * channels + 16),
            transcendentals=rows,
            bytes_accessed=4 * rows * width,
        ),
        name="normed_rows",
    )(latent, embed, stream, gain, shift)


def placed_kernel(spots, *refs):
    pieces, (out_ref, zeros, sem) = refs[:-3], refs[-3:]
    x, z = spots[0], spots[1]
    depth = out_ref.shape[0] // (NX * NZ)
    late = depth - SPLIT
    half_late = late // 2
    copies = []

    def put(source, hop_x, hop_z, start, rows):
        place = lax.rem(x + hop_x, NX) * NZ + lax.rem(z + hop_z, NZ)
        spot = pl.ds(pl.multiple_of(place * depth + start, 16), rows)
        copy = pltpu.make_async_copy(source, out_ref.at[spot, :], sem.at[len(copies)])
        copy.start()
        copies.append(copy)

    def take(piece, row, hop_x, hop_z, start, rows):
        put(pieces[piece].at[pl.ds(row, rows), :], hop_x, hop_z, start, rows)

    own, left3, right3, left4, right4, left5, right5 = range(7)
    near, near_right, near_left, near_low, near_high = range(7, 12)
    rest, rest_right, rest_left = range(12, 15)
    hops = ((own, 0), (right3, 1), (right4, 2), (right5, 3), (left5, 5), (left4, 6), (left3, 7))
    zeros[...] = jnp.zeros_like(zeros)
    for hop_x in range(NX):
        for piece, hop in hops:
            take(piece, hop_x * SPLIT, hop_x, hop, 0, SPLIT)
        put(zeros.at[pl.ds(0, SPLIT), :], hop_x, NZ // 2, 0, SPLIT)
        for i, hop in enumerate(NEAR):
            if hop_x == 2:
                piece, row = (near_low, i) if i < 3 else (near_high, i - 3)
            else:
                piece, row = (near, near_right, None, near_left)[hop_x], i
            take(piece, row * late, hop_x, hop, SPLIT, late)
        for i, hop in enumerate(REST):
            if hop_x == 2:
                put(zeros.at[pl.ds(0, late), :], hop_x, hop, SPLIT, late)
            else:
                piece = (rest, rest_right, None, rest_left)[hop_x]
                take(piece, i * late, hop_x, hop, SPLIT, late)
    for copy in copies:
        copy.wait()


NEAR = (0, 1, 2, 6, 7)
REST = (3, 4, 5)
COPIES = NX * (NZ + len(NEAR) + len(REST))


def placed(pieces, width):
    columns = pieces[0].shape[1]
    late = width // (NX * NZ) - SPLIT
    place = lax.axis_index("tm")
    spots = jnp.stack([place // NZ, lax.rem(place, NZ)]).astype(jnp.int32)
    return pl.pallas_call(
        placed_kernel,
        grid_spec=pltpu.PrefetchScalarGridSpec(
            num_scalar_prefetch=1,
            grid=(1,),
            in_specs=[pl.BlockSpec(memory_space=pl.ANY)] * len(pieces),
            out_specs=pl.BlockSpec(memory_space=pltpu.VMEM),
            scratch_shapes=[
                pltpu.VMEM((max(SPLIT, late), columns), jnp.bfloat16),
                pltpu.SemaphoreType.DMA((COPIES,)),
            ],
        ),
        out_shape=jax.ShapeDtypeStruct((width, columns), jnp.bfloat16),
        cost_estimate=pl.CostEstimate(
            flops=0, transcendentals=0, bytes_accessed=4 * width * columns
        ),
        compiler_params=pltpu.CompilerParams(vmem_limit_bytes=32 * 2**20),
        name="placed",
    )(spots, *pieces)


def moved(sends, *others):
    arrived = [move(value, hop) for value, move, hop in sends]
    return lax.optimization_barrier((*arrived, *others))


def spread_kernel(core_ref, act_ref, down_ref, keep_ref, away_ref):
    full = lax.dot_general(
        act_ref[...],
        down_ref[...],
        (((1,), (1,)), ((), ())),
        preferred_element_type=jnp.float32,
    )
    even_mine = core_ref[0] == 0
    rows = keep_ref.shape[1]
    for y in range(NY):
        even = full[2 * y * rows : (2 * y + 1) * rows]
        odd = full[(2 * y + 1) * rows : (2 * y + 2) * rows]
        keep_ref[y] = jnp.where(even_mine, even, odd).astype(keep_ref.dtype)
        away_ref[y] = jnp.where(even_mine, odd, even).astype(away_ref.dtype)


def spread(activated, down, core, start, count):
    rows, units = activated.shape
    own = rows // (2 * NY)
    per = 640
    shape = jax.ShapeDtypeStruct((NY, own, count), jnp.bfloat16)
    block = pl.BlockSpec((NY, own, per), lambda i, core: (0, 0, i))
    return pl.pallas_call(
        spread_kernel,
        grid_spec=pltpu.PrefetchScalarGridSpec(
            num_scalar_prefetch=1,
            grid=(count // per,),
            in_specs=[
                pl.BlockSpec((rows, units), lambda i, core: (0, 0)),
                pl.BlockSpec((per, units), lambda i, core: (start // per + i, 0)),
            ],
            out_specs=[block, block],
        ),
        out_shape=(shape, shape),
        compiler_params=pltpu.CompilerParams(vmem_limit_bytes=24 * 2**20),
        cost_estimate=pl.CostEstimate(
            flops=2 * rows * units * count,
            transcendentals=0,
            bytes_accessed=2 * (rows * units + units * count + rows * count),
        ),
        name="spread",
    )(core[None].astype(jnp.int32), activated, down)


def total_over_chips(both, y):
    half = both.shape[-1] // 2

    def block(hop):
        return lax.dynamic_index_in_dim(both, lax.rem(y + hop, NY), 0, False)

    far = block(2).astype(jnp.bfloat16)
    low = send_y(far[:, :half], 1).astype(jnp.float32)
    high = send_y(far[:, half:], -1).astype(jnp.float32)
    ahead, behind = block(1), block(3)
    ahead = jnp.concatenate([ahead[:, :half] + low, ahead[:, half:]], axis=1)
    behind = jnp.concatenate([behind[:, :half], behind[:, half:] + high], axis=1)
    ahead = send_y(ahead.astype(jnp.bfloat16), 1).astype(jnp.float32)
    behind = send_y(behind.astype(jnp.bfloat16), -1).astype(jnp.float32)
    return block(0) + ahead + behind


def running_sum(term, x, z):
    before, after, far = send_x(term, 1), send_x(term, -1), send_x(term, 2)
    zero = jnp.zeros_like(term)
    whole = (
        jnp.where(x >= 1, before, zero)
        + jnp.where(x >= 2, far, zero)
        + jnp.where(x >= 3, after, zero)
    )
    mine = jnp.stack([whole, term])
    behind, ahead = send_z(mine, 1), send_z(mine, -1)
    triple = [(-1, behind), (0, mine), (1, ahead)]

    def share(pair, source, target):
        return pair[0] + jnp.where(source <= target, pair[1], jnp.zeros_like(term))

    def place(hop):
        return lax.rem(z + hop + 2 * NZ, NZ)

    up = sum(share(pair, place(d), place(3)) for d, pair in triple)
    down = sum(share(pair, place(d), place(-3)) for d, pair in triple if d != 1)
    total = share(mine, z, z) + share(behind, place(-1), z) + share(ahead, place(1), z)
    return total + send_z(up, 3) + send_z(down, -3)


def local(
    latents,
    residual,
    timesteps,
    step_sizes,
    embed_weight,
    mod_weight,
    up_weight,
    down_weight,
    head_weight,
):
    latent = latents[0]
    stream = residual[0]
    own_rows, channels = latent.shape
    width = stream.shape[1]
    depth, hidden_units = up_weight.shape
    place = lax.axis_index("tm")
    x, z = place // NZ, lax.rem(place, NZ)
    member = lax.axis_index("tensor")
    y, core = member // 2, lax.rem(member, 2)

    down = lax.all_gather(down_weight.T, "tm", axis=0)

    late = depth - SPLIT
    first, second = up_weight[:SPLIT], up_weight[SPLIT:]

    feature = jax.nn.silu(time_features(timesteps, mod_weight.shape[1])).astype(jnp.bfloat16)[0]
    piece_mod = jnp.einsum("f,kfd->kd", feature, mod_weight, preferred_element_type=jnp.float32)
    own = jnp.concatenate([piece_mod.reshape(-1), latent.reshape(-1)]).reshape(-1, 128)

    a_left, a_right, b_left1, b_right1, own, first, second = moved(
        [(first, send_x, 1), (first, send_x, -1), (second, send_z, 1), (second, send_z, -1)],
        own,
        first,
        second,
    )
    a_low, a_high, b_left2, b_right2, own = moved(
        [
            (a_left[: SPLIT // 2], send_x, 1),
            (a_right[SPLIT // 2 :], send_x, -1),
            (b_left1, send_z, 1),
            (b_right1, send_z, -1),
        ],
        own,
    )
    block = jnp.concatenate([first, a_right, a_low, a_high, a_left], axis=0)
    near = jnp.concatenate([second, b_right1, b_right2, b_left2, b_left1], axis=0)
    left3 = jnp.concatenate([block, b_left2], axis=0)
    right3 = jnp.concatenate([block, b_right2], axis=0)
    block, near, left3, right3 = lax.optimization_barrier((block, near, left3, right3))
    shared = lax.all_gather(own, "tensor", axis=0)
    left3, right3, near_left, near_right, shared = moved(
        [
            (left3, send_z, 1),
            (right3, send_z, -1),
            (near, send_x, 1),
            (near, send_x, -1),
        ],
        shared,
    )
    shared = shared.reshape(8, -1)
    cut = piece_mod.size
    modulation = shared[:, :cut].reshape(8, 3, -1).transpose(1, 0, 2).reshape(3, width)
    all_latent = shared[:, cut:].reshape(8 * own_rows, channels).astype(jnp.bfloat16)
    gain, shift = 1.0 + modulation[1][None], modulation[0][None]
    held = pltpu.with_memory_space_constraint(stream, pltpu.HBM)
    normed = normed_rows(all_latent, embed_weight, held, gain, shift)
    span = NX * SPLIT
    left4, right4, near_low, near_high, normed = moved(
        [
            (left3[: span + late // 2], send_z, 1),
            (
                jnp.concatenate([right3[:span], right3[span + late // 2 :]], axis=0),
                send_z,
                -1,
            ),
            (near_left[: 3 * late], send_x, 1),
            (near_right[3 * late :], send_x, -1),
        ],
        normed,
    )
    rest = jnp.concatenate([right3[span:], left4[span:], right4[span:], left3[span:]], axis=0)
    left5, right5, rest_left, rest_right = moved(
        [
            (left4[:span], send_z, 1),
            (right4[:span], send_z, -1),
            (rest, send_x, 1),
            (rest, send_x, -1),
        ],
    )

    def halves(rows, start):
        cut_rows = rows.reshape(3, late, hidden_units)[:, start : start + late // 2]
        return cut_rows.reshape(3 * late // 2, hidden_units)

    pieces = [block, left3, right3, left4, right4, left5, right5]
    pieces += [near, near_right, near_left, near_low, near_high]
    pieces += [rest, rest_right, rest_left]
    preact = jnp.dot(normed, placed(pieces, width), preferred_element_type=jnp.float32)

    def columns(hop_x, hop_z, start, count):
        shard = lax.rem(x + hop_x, NX) * NZ + lax.rem(z + hop_z, NZ)
        return lax.dynamic_slice_in_dim(normed, shard * depth + start, count, 1)

    missing = [columns(hop_x, NZ // 2, 0, SPLIT) for hop_x in range(NX)]
    for start in (SPLIT, SPLIT + late // 2):
        missing += [columns(2, hop, start, late // 2) for hop in REST]
    missing = jnp.concatenate(missing, axis=1)
    left6, right6, rest_low, rest_high, preact, missing = moved(
        [
            (left5[: span // 2], send_z, 1),
            (right5[span // 2 :], send_z, -1),
            (halves(rest_left, 0), send_x, 1),
            (halves(rest_right, late // 2), send_x, -1),
        ],
        preact,
        missing,
    )
    last = jnp.concatenate([left6, right6, rest_low, rest_high], axis=0)
    preact = preact + jnp.dot(missing, last, preferred_element_type=jnp.float32)
    activated = jax.nn.gelu(preact, approximate=True).astype(jnp.bfloat16)

    own_stream = lax.dynamic_slice_in_dim(stream, member * own_rows, own_rows, 0)
    hidden = own_stream.astype(jnp.float32) + jnp.dot(
        latent.astype(jnp.bfloat16), embed_weight, preferred_element_type=jnp.float32
    )

    totals = []
    start = 0
    down = down.reshape(width, hidden_units)
    down = pltpu.with_memory_space_constraint(down, pltpu.HBM)
    for shards in CHUNKS:
        count = shards * depth
        keep, away = spread(activated, down, core, start, count)
        start += count
        both = keep.astype(jnp.float32) + send_core(away).astype(jnp.float32)
        totals.append(total_over_chips(both, y))
    mixed = jnp.concatenate(totals, axis=1)
    updated = hidden + modulation[2] * mixed
    drift = jnp.dot(
        normalize(updated).astype(jnp.bfloat16), head_weight, preferred_element_type=jnp.float32
    )
    first = (place == 0).astype(jnp.float32)
    new_latent = running_sum(first * latent - step_sizes[0] * drift, x, z)
    return (drift[None], new_latent[None])


def solution(mesh):
    in_specs = (
        P("tm", "tensor", None),
        P("tm", None, None),
        P("tm"),
        P("tm"),
        P(),
        P(None, None, "tensor"),
        P("tm", "tensor"),
        P("tensor", "tm"),
        P(),
    )
    out_specs = (P("tm", "tensor", None), P("tm", "tensor", None))
    return jax.shard_map(local, mesh=mesh, in_specs=in_specs, out_specs=out_specs, check_vma=False)
```

```python
import math

import jax
import jax.numpy as jnp
from jax import lax
from jax.experimental import pallas as pl
from jax.experimental.pallas import tpu as pltpu
from jax.sharding import PartitionSpec as P

NX, NZ, NY = 4, 8, 4
SPLIT = 64
CHUNKS = (16, 16)


def normalize(values):
    centre = values - jnp.mean(values, axis=-1, keepdims=True)
    spread = jnp.mean(centre * centre, axis=-1, keepdims=True)
    return centre * lax.rsqrt(spread + 1e-06)


def time_features(stamps, width):
    half = width // 2
    freqs = jnp.exp(-math.log(10000.0) * jnp.arange(half, dtype=jnp.float32) / half)
    angles = stamps.astype(jnp.float32)[:, None] * freqs[None, :]
    return jnp.concatenate([jnp.cos(angles), jnp.sin(angles)], axis=-1)


def send_x(value, hop):
    pairs = [(x * NZ + z, (x + hop) % NX * NZ + z) for x in range(NX) for z in range(NZ)]
    return lax.ppermute(value, "tm", pairs)


def send_z(value, hop):
    pairs = [(x * NZ + z, x * NZ + (z + hop) % NZ) for x in range(NX) for z in range(NZ)]
    return lax.ppermute(value, "tm", pairs)


def send_y(value, hop):
    pairs = [(y * 2 + c, (y + hop) % NY * 2 + c) for y in range(NY) for c in range(2)]
    return lax.ppermute(value, "tensor", pairs)


def send_core(value):
    pairs = [(y * 2 + c, y * 2 + 1 - c) for y in range(NY) for c in range(2)]
    return lax.ppermute(value, "tensor", pairs)


def after(values, done):
    count = len(values)
    return lax.optimization_barrier((*values, *done))[:count]


def normed_kernel(latent_ref, embed_ref, stream_ref, gain_ref, shift_ref, out_ref):
    values = stream_ref[...].astype(jnp.float32) + jnp.dot(
        latent_ref[...], embed_ref[...], preferred_element_type=jnp.float32
    )
    scaled = normalize(values) * gain_ref[...] + shift_ref[...]
    out_ref[...] = scaled.astype(out_ref.dtype)


def normed_rows(latent, embed, stream, gain, shift):
    rows, width = stream.shape
    channels = latent.shape[1]
    per = 80
    return pl.pallas_call(
        normed_kernel,
        grid=(rows // per,),
        in_specs=[
            pl.BlockSpec((per, channels), lambda i: (i, 0)),
            pl.BlockSpec((channels, width), lambda i: (0, 0)),
            pl.BlockSpec((per, width), lambda i: (i, 0)),
            pl.BlockSpec((1, width), lambda i: (0, 0)),
            pl.BlockSpec((1, width), lambda i: (0, 0)),
        ],
        out_specs=pl.BlockSpec((per, width), lambda i: (i, 0)),
        out_shape=jax.ShapeDtypeStruct((rows, width), jnp.bfloat16),
        compiler_params=pltpu.CompilerParams(vmem_limit_bytes=24 * 2**20),
        cost_estimate=pl.CostEstimate(
            flops=rows * width * (2 * channels + 16),
            transcendentals=rows,
            bytes_accessed=4 * rows * width,
        ),
        name="normed_rows",
    )(latent, embed, stream, gain, shift)


def placed_kernel(spots, *refs):
    pieces, (out_ref, zeros, sem) = refs[:-3], refs[-3:]
    x, z = spots[0], spots[1]
    depth = out_ref.shape[0] // (NX * NZ)
    late = depth - SPLIT
    half_late = late // 2
    copies = []

    def put(source, hop_x, hop_z, start, rows):
        place = lax.rem(x + hop_x, NX) * NZ + lax.rem(z + hop_z, NZ)
        spot = pl.ds(pl.multiple_of(place * depth + start, 16), rows)
        copy = pltpu.make_async_copy(source, out_ref.at[spot, :], sem.at[len(copies)])
        copy.start()
        copies.append(copy)

    def take(piece, row, hop_x, hop_z, start, rows):
        put(pieces[piece].at[pl.ds(row, rows), :], hop_x, hop_z, start, rows)

    own, left3, right3, left4, right4, left5, right5 = range(7)
    near, near_right, near_left, near_low, near_high = range(7, 12)
    rest, rest_right, rest_left = range(12, 15)
    hops = ((own, 0), (right3, 1), (right4, 2), (right5, 3), (left5, 5), (left4, 6), (left3, 7))
    zeros[...] = jnp.zeros_like(zeros)
    for hop_x in range(NX):
        for piece, hop in hops:
            take(piece, hop_x * SPLIT, hop_x, hop, 0, SPLIT)
        put(zeros.at[pl.ds(0, SPLIT), :], hop_x, NZ // 2, 0, SPLIT)
        for i, hop in enumerate(NEAR):
            if hop_x == 2:
                piece, row = (near_low, i) if i < 3 else (near_high, i - 3)
            else:
                piece, row = (near, near_right, None, near_left)[hop_x], i
            take(piece, row * late, hop_x, hop, SPLIT, late)
        for i, hop in enumerate(REST):
            if hop_x == 2:
                put(zeros.at[pl.ds(0, late), :], hop_x, hop, SPLIT, late)
            else:
                piece = (rest, rest_right, None, rest_left)[hop_x]
                take(piece, i * late, hop_x, hop, SPLIT, late)
    for copy in copies:
        copy.wait()


NEAR = (0, 1, 2, 6, 7)
REST = (3, 4, 5)
COPIES = NX * (NZ + len(NEAR) + len(REST))


def placed(pieces, width):
    columns = pieces[0].shape[1]
    late = width // (NX * NZ) - SPLIT
    place = lax.axis_index("tm")
    spots = jnp.stack([place // NZ, lax.rem(place, NZ)]).astype(jnp.int32)
    return pl.pallas_call(
        placed_kernel,
        grid_spec=pltpu.PrefetchScalarGridSpec(
            num_scalar_prefetch=1,
            grid=(1,),
            in_specs=[pl.BlockSpec(memory_space=pl.ANY)] * len(pieces),
            out_specs=pl.BlockSpec(memory_space=pltpu.VMEM),
            scratch_shapes=[
                pltpu.VMEM((max(SPLIT, late), columns), jnp.bfloat16),
                pltpu.SemaphoreType.DMA((COPIES,)),
            ],
        ),
        out_shape=jax.ShapeDtypeStruct((width, columns), jnp.bfloat16),
        cost_estimate=pl.CostEstimate(
            flops=0, transcendentals=0, bytes_accessed=4 * width * columns
        ),
        compiler_params=pltpu.CompilerParams(vmem_limit_bytes=32 * 2**20),
        name="placed",
    )(spots, *pieces)


def moved(sends, *others):
    arrived = [move(value, hop) for value, move, hop in sends]
    return lax.optimization_barrier((*arrived, *others))


def spread_kernel(core_ref, act_ref, down_ref, keep_ref, away_ref):
    full = lax.dot_general(
        act_ref[...],
        down_ref[...],
        (((1,), (1,)), ((), ())),
        preferred_element_type=jnp.float32,
    )
    even_mine = core_ref[0] == 0
    rows = keep_ref.shape[1]
    for y in range(NY):
        even = full[2 * y * rows : (2 * y + 1) * rows]
        odd = full[(2 * y + 1) * rows : (2 * y + 2) * rows]
        keep_ref[y] = jnp.where(even_mine, even, odd).astype(keep_ref.dtype)
        away_ref[y] = jnp.where(even_mine, odd, even).astype(away_ref.dtype)


def spread(activated, down, core, start, count):
    rows, units = activated.shape
    own = rows // (2 * NY)
    per = 640
    shape = jax.ShapeDtypeStruct((NY, own, count), jnp.bfloat16)
    block = pl.BlockSpec((NY, own, per), lambda i, core: (0, 0, i))
    return pl.pallas_call(
        spread_kernel,
        grid_spec=pltpu.PrefetchScalarGridSpec(
            num_scalar_prefetch=1,
            grid=(count // per,),
            in_specs=[
                pl.BlockSpec((rows, units), lambda i, core: (0, 0)),
                pl.BlockSpec((per, units), lambda i, core: (start // per + i, 0)),
            ],
            out_specs=[block, block],
        ),
        out_shape=(shape, shape),
        compiler_params=pltpu.CompilerParams(vmem_limit_bytes=24 * 2**20),
        cost_estimate=pl.CostEstimate(
            flops=2 * rows * units * count,
            transcendentals=0,
            bytes_accessed=2 * (rows * units + units * count + rows * count),
        ),
        name="spread",
    )(core[None].astype(jnp.int32), activated, down)


def total_over_chips(both, y):
    half = both.shape[-1] // 2

    def block(hop):
        return lax.dynamic_index_in_dim(both, lax.rem(y + hop, NY), 0, False)

    far = block(2).astype(jnp.bfloat16)
    low = send_y(far[:, :half], 1).astype(jnp.float32)
    high = send_y(far[:, half:], -1).astype(jnp.float32)
    ahead, behind = block(1), block(3)
    ahead = jnp.concatenate([ahead[:, :half] + low, ahead[:, half:]], axis=1)
    behind = jnp.concatenate([behind[:, :half], behind[:, half:] + high], axis=1)
    ahead = send_y(ahead.astype(jnp.bfloat16), 1).astype(jnp.float32)
    behind = send_y(behind.astype(jnp.bfloat16), -1).astype(jnp.float32)
    return block(0) + ahead + behind


def running_sum(term, x, z):
    before, after, far = send_x(term, 1), send_x(term, -1), send_x(term, 2)
    zero = jnp.zeros_like(term)
    whole = (
        jnp.where(x >= 1, before, zero)
        + jnp.where(x >= 2, far, zero)
        + jnp.where(x >= 3, after, zero)
    )
    mine = jnp.stack([whole, term])
    behind, ahead = send_z(mine, 1), send_z(mine, -1)
    triple = [(-1, behind), (0, mine), (1, ahead)]

    def share(pair, source, target):
        return pair[0] + jnp.where(source <= target, pair[1], jnp.zeros_like(term))

    def place(hop):
        return lax.rem(z + hop + 2 * NZ, NZ)

    up = sum(share(pair, place(d), place(3)) for d, pair in triple)
    down = sum(share(pair, place(d), place(-3)) for d, pair in triple if d != 1)
    total = share(mine, z, z) + share(behind, place(-1), z) + share(ahead, place(1), z)
    return total + send_z(up, 3) + send_z(down, -3)


def local(
    latents,
    residual,
    timesteps,
    step_sizes,
    embed_weight,
    mod_weight,
    up_weight,
    down_weight,
    head_weight,
):
    latent = latents[0]
    stream = residual[0]
    own_rows, channels = latent.shape
    width = stream.shape[1]
    depth, hidden_units = up_weight.shape
    place = lax.axis_index("tm")
    x, z = place // NZ, lax.rem(place, NZ)
    member = lax.axis_index("tensor")
    y, core = member // 2, lax.rem(member, 2)

    down = lax.all_gather(down_weight.T, "tm", axis=0)

    late = depth - SPLIT
    first, second = up_weight[:SPLIT], up_weight[SPLIT:]

    feature = jax.nn.silu(time_features(timesteps, mod_weight.shape[1])).astype(jnp.bfloat16)[0]
    piece_mod = jnp.einsum("f,kfd->kd", feature, mod_weight, preferred_element_type=jnp.float32)
    own = jnp.concatenate([piece_mod.reshape(-1), latent.reshape(-1)]).reshape(-1, 128)

    a_left, a_right, b_left1, b_right1, own, first, second = moved(
        [(first, send_x, 1), (first, send_x, -1), (second, send_z, 1), (second, send_z, -1)],
        own,
        first,
        second,
    )
    a_low, a_high, b_left2, b_right2, own = moved(
        [
            (a_left[: SPLIT // 2], send_x, 1),
            (a_right[SPLIT // 2 :], send_x, -1),
            (b_left1, send_z, 1),
            (b_right1, send_z, -1),
        ],
        own,
    )
    block = jnp.concatenate([first, a_right, a_low, a_high, a_left], axis=0)
    near = jnp.concatenate([second, b_right1, b_right2, b_left2, b_left1], axis=0)
    left3 = jnp.concatenate([block, b_left2], axis=0)
    right3 = jnp.concatenate([block, b_right2], axis=0)
    block, near, left3, right3 = lax.optimization_barrier((block, near, left3, right3))
    shared = lax.all_gather(own, "tensor", axis=0)
    left3, right3, near_left, near_right, shared = moved(
        [
            (left3, send_z, 1),
            (right3, send_z, -1),
            (near, send_x, 1),
            (near, send_x, -1),
        ],
        shared,
    )
    shared = shared.reshape(8, -1)
    cut = piece_mod.size
    modulation = shared[:, :cut].reshape(8, 3, -1).transpose(1, 0, 2).reshape(3, width)
    all_latent = shared[:, cut:].reshape(8 * own_rows, channels).astype(jnp.bfloat16)
    gain, shift = 1.0 + modulation[1][None], modulation[0][None]
    held = pltpu.with_memory_space_constraint(stream, pltpu.HBM)
    normed = normed_rows(all_latent, embed_weight, held, gain, shift)
    span = NX * SPLIT
    left4, right4, near_low, near_high, normed = moved(
        [
            (left3[: span + late // 2], send_z, 1),
            (
                jnp.concatenate([right3[:span], right3[span + late // 2 :]], axis=0),
                send_z,
                -1,
            ),
            (near_left[: 3 * late], send_x, 1),
            (near_right[3 * late :], send_x, -1),
        ],
        normed,
    )
    rest = jnp.concatenate([right3[span:], left4[span:], right4[span:], left3[span:]], axis=0)
    left5, right5, rest_left, rest_right = moved(
        [
            (left4, send_z, 1),
            (right4, send_z, -1),
            (rest, send_x, 1),
            (rest, send_x, -1),
        ],
    )

    def halves(rows, start):
        cut_rows = rows.reshape(3, late, hidden_units)[:, start : start + late // 2]
        return cut_rows.reshape(3 * late // 2, hidden_units)

    pieces = [block, left3, right3, left4, right4, left5, right5]
    pieces += [near, near_right, near_left, near_low, near_high]
    pieces += [rest, rest_right, rest_left]
    preact = jnp.dot(normed, placed(pieces, width), preferred_element_type=jnp.float32)

    def columns(hop_x, hop_z, start, count):
        shard = lax.rem(x + hop_x, NX) * NZ + lax.rem(z + hop_z, NZ)
        return lax.dynamic_slice_in_dim(normed, shard * depth + start, count, 1)

    missing = [columns(hop_x, NZ // 2, 0, SPLIT) for hop_x in range(NX)]
    for start in (SPLIT, SPLIT + late // 2):
        missing += [columns(2, hop, start, late // 2) for hop in REST]
    missing = jnp.concatenate(missing, axis=1)
    left6, right6, rest_low, rest_high, preact, missing = moved(
        [
            (left5[: span // 2], send_z, 1),
            (right5[span // 2 : span], send_z, -1),
            (halves(rest_left, 0), send_x, 1),
            (halves(rest_right, late // 2), send_x, -1),
        ],
        preact,
        missing,
    )
    last = jnp.concatenate([left6, right6, rest_low, rest_high], axis=0)
    preact = preact + jnp.dot(missing, last, preferred_element_type=jnp.float32)
    activated = jax.nn.gelu(preact, approximate=True).astype(jnp.bfloat16)

    own_stream = lax.dynamic_slice_in_dim(stream, member * own_rows, own_rows, 0)
    hidden = own_stream.astype(jnp.float32) + jnp.dot(
        latent.astype(jnp.bfloat16), embed_weight, preferred_element_type=jnp.float32
    )

    totals = []
    start = 0
    down = down.reshape(width, hidden_units)
    down = pltpu.with_memory_space_constraint(down, pltpu.HBM)
    for shards in CHUNKS:
        count = shards * depth
        keep, away = spread(activated, down, core, start, count)
        start += count
        both = keep.astype(jnp.float32) + send_core(away).astype(jnp.float32)
        totals.append(total_over_chips(both, y))
    mixed = jnp.concatenate(totals, axis=1)
    updated = hidden + modulation[2] * mixed
    drift = jnp.dot(
        normalize(updated).astype(jnp.bfloat16), head_weight, preferred_element_type=jnp.float32
    )
    first = (place == 0).astype(jnp.float32)
    new_latent = running_sum(first * latent - step_sizes[0] * drift, x, z)
    return (drift[None], new_latent[None])


def solution(mesh):
    in_specs = (
        P("tm", "tensor", None),
        P("tm", None, None),
        P("tm"),
        P("tm"),
        P(),
        P(None, None, "tensor"),
        P("tm", "tensor"),
        P("tensor", "tm"),
        P(),
    )
    out_specs = (P("tm", "tensor", None), P("tm", "tensor", None))
    return jax.shard_map(local, mesh=mesh, in_specs=in_specs, out_specs=out_specs, check_vma=False)
```
